512 devices in a mesh: ab: 16 (over z, core), cd: 8 (over y), rep: 4 (over x).
Axes of the slice: x: 4, y: 8, z: 8, core: 2. Of those that a mesh axis runs over, the one named last changes fastest.
Arguments:
- amplitudes: bfloat16 [4, 2048, 8192], P('rep', 'ab', 'cd'), may hold values from -6 to 6
- pair_irrep: int32 [4, 2048], P('rep', 'ab'), may hold values from 0 to 7, as said below
- integrals: bfloat16 [8192, 8192], P('ab', 'cd'), may hold values from -0.0625 to 0.0625
- residual_in: bfloat16 [4, 2048, 8192], P('rep', None, ('ab', 'cd')), may hold values from -6 to 6
Outputs:
- residual: bfloat16 [4, 2048, 8192], P('rep', None, ('ab', 'cd'))
The draws below stay inside these ranges and needn't reach their ends.
Inputs may be any that keep to these rules, and one draw needn't show every extreme that they name: For each j, among the 512 labels pair_irrep(l, j * 128 + t) over all layers l and 0 <= t < 128, exactly half are 0, and in one layer l (drawn) all 128 of them are 0.
All inputs are finite; a program needn't handle non-finite values.
Results may differ from the reference program's by a relative error of at most 0.001.
Values may be sent and summed in bfloat16 or wider, within the bound.
No kernel may reach another device: no remote copies, remote signals or barrier semaphores. Data moves between devices by JAX's collectives and lax.ppermute only.
A program may use at most 64 MiB of HBM per device.

```python
import jax
import jax.numpy as jnp
from jax import lax

CD = 8192
IRREPS = 8
PAIR_DEV = 128
LAYERS = 4
PAIRS_L = 2048
AB = 8192


def draw_pair_irrep(key, part):
    slab_total = PAIRS_L // PAIR_DEV
    others = (LAYERS - 1) * PAIR_DEV
    needed = LAYERS * PAIR_DEV // 2 - PAIR_DEV
    key_busy, key_pick, key_label = jax.random.split(key, 3)
    busy = jax.random.randint(key_busy, (slab_total,), 0, LAYERS)

    def draw_one(sub_key):
        return jax.random.permutation(sub_key, others)
    picks = jax.vmap(draw_one)(jax.random.split(key_pick, slab_total))
    chosen = picks < needed
    layer_ids = jnp.arange(LAYERS)[:, None]
    within = jnp.arange(PAIR_DEV)[None, :]

    def one_slab(busy_layer, chosen_row):
        shifted = layer_ids - (layer_ids > busy_layer).astype(jnp.int32)
        position = jnp.clip(shifted * PAIR_DEV + within, 0, others - 1)
        return jnp.where(layer_ids == busy_layer, True, chosen_row[position])
    marked = jax.vmap(one_slab)(busy, chosen)
    spare = jax.random.randint(key_label, marked.shape, 1, IRREPS)
    labels = jnp.where(marked, 0, spare)
    return jnp.transpose(labels, (1, 0, 2)).reshape(LAYERS, PAIRS_L).astype(jnp.int32)


def steps_of(stream_key, extent, pieces, least, largest):
    def one(dim, shards_of):
        heights = jax.random.uniform(jax.random.fold_in(jax.random.fold_in(stream_key, 6), dim), (shards_of,), jnp.float32, least / len(pieces), largest / len(pieces))
        return jnp.repeat(jnp.exp(heights), extent[dim] // shards_of).reshape((-1,) + (1,) * (len(extent) - dim - 1))

    loudness = one(*pieces[0])
    for cut in pieces[1:]:
        loudness = loudness * one(*cut)
    return loudness


def normal_values(rng, shape, deviation, reach, pieces=(), kind=jnp.bfloat16):
    drawn = jax.random.normal(rng, shape, jnp.float32) * deviation
    if len(pieces) > 0:
        drawn = steps_of(rng, shape, pieces, -0.22, 0.18) * drawn
    return jnp.clip(drawn, min=-reach, max=reach).astype(kind)


def setup_inputs(seed: int = 0) -> dict:
    splits = jax.random.split(jax.random.key(seed), 5)
    amplitudes = normal_values(splits[0], (LAYERS, PAIRS_L, CD), 1.0, 6.0, ((0, 4), (1, 16), (2, 8)))
    pair_irrep = draw_pair_irrep(jax.random.fold_in(splits[4], 71), 0)
    integrals = normal_values(splits[2], (AB, CD), CD ** -0.5, 0.0625, ((0, 16), (1, 8)))
    residual_in = normal_values(splits[3], (LAYERS, PAIRS_L, AB), 1.0, 6.0, ((0, 4), (2, 128)))
    return {"amplitudes": amplitudes, "pair_irrep": pair_irrep, "integrals": integrals, "residual_in": residual_in}


def reference(amplitudes, pair_irrep, integrals, residual_in):
    def one_layer(inputs):
        layer_amps, layer_labels, layer_res = inputs
        ladder = jnp.dot(layer_amps, integrals.T, preferred_element_type=jnp.float32)
        active = (layer_labels == 0).astype(jnp.float32)[:, None]
        return (layer_res.astype(jnp.float32) + active * ladder).astype(jnp.bfloat16)

    return lax.map(one_layer, (amplitudes, pair_irrep, residual_in))
```

```python
import jax
import jax.numpy as jnp
from jax import lax
from jax.sharding import Mesh, PartitionSpec as P


def local(amplitudes, pair_irrep, integrals, residual_in):
    keep = (pair_irrep[0] == 0)[:, None]
    rows = jnp.where(keep, amplitudes[0], jnp.zeros((), amplitudes.dtype))

    halves = jnp.broadcast_to(rows.reshape(2, 1, 64, 1024), (2, 8, 64, 1024))
    got = lax.all_to_all(halves.reshape(16, 64, 1024), ("b", "z"), 0, 0, tiled=True)
    got = got.reshape(2, 512, 1024)

    b = lax.axis_index("b")
    k = lax.axis_index("k")
    swap = [(0, 1), (1, 0)]
    other = lax.ppermute(integrals, "b", swap)
    low = jnp.where(b == 0, integrals, other)
    high = jnp.where(b == 0, other, integrals)
    wide = jnp.stack([low, high])
    across = lax.ppermute(wide, "k", swap)
    first = jnp.where(k == 0, wide, across)
    second = jnp.where(k == 0, across, wide)
    full = jnp.concatenate([first, second], axis=1)

    dims = (((1,), (1,)), ((), ()))
    partial = lax.dot_general(full[0], got[0], dims, preferred_element_type=jnp.float32)
    partial += lax.dot_general(full[1], got[1], dims, preferred_element_type=jnp.float32)

    sent = partial.astype(jnp.float16).reshape(16, 64, 512)
    parts = lax.all_to_all(sent, ("k", "g", "b"), 0, 0, tiled=True)
    summed = jnp.sum(parts.reshape(2, 4, 2, 64, 8, 64).astype(jnp.float32), axis=1)
    ladder = jnp.transpose(summed, (3, 0, 1, 4, 2)).reshape(2048, 64)
    return (residual_in[0].astype(jnp.float32) + ladder).astype(jnp.bfloat16)[None]


def solution(mesh):
    devices = mesh.devices.reshape(8, 2, 4, 2, 4)
    split = Mesh(devices, ("z", "k", "g", "b", "rep"))
    ab, cd = ("z", "k"), ("g", "b")
    return jax.shard_map(
        local,
        mesh=split,
        in_specs=(P("rep", ab, cd), P("rep", ab), P(ab, cd), P("rep", None, ab + cd)),
        out_specs=P("rep", None, ab + cd),
        check_vma=False,
    )
```

```python
import jax
import jax.numpy as jnp
from jax import lax
from jax.experimental import pallas as pl
from jax.experimental.pallas import tpu as pltpu
from jax.sharding import Mesh, PartitionSpec as P


LAYERS = 4
T = 128
KD = 1024
CLASSES = 8
SEND = 24
BASE = 16
SHARE = 32
Z = 8
ROWS = Z * BASE
i32, f32, bf16 = jnp.int32, jnp.float32, jnp.bfloat16


def iota(shape, dim):
    return lax.broadcasted_iota(i32, shape, dim)


def ranks(active):
    before = (iota((T, T), 0) < iota((T, T), 1)).astype(bf16)
    return jnp.dot(active.astype(bf16), before, preferred_element_type=f32).astype(i32)


def pack_kernel(labels_ref, rows_ref, out_ref):
    active = jnp.broadcast_to(labels_ref[...] == 0, (8, T)).astype(i32).astype(f32)
    rank = jnp.where(active[:1] > 0, ranks(active)[:1], -1)
    count = jnp.sum(active, axis=1, keepdims=True).astype(i32)[:1]
    even = (count >> 3) << 3
    rows = rows_ref[...]
    slot = iota((SEND, T), 0)
    lane = iota((SEND, KD), 1)
    srow = iota((SEND, KD), 0)
    flags = jnp.concatenate([active[:1]] * (KD // T), axis=1)
    info = jnp.where(lane < T, flags, count.astype(f32))
    for q in range(CLASSES):
        shared = 8 * slot + q
        rest = even + slot - BASE
        target = jnp.where(slot < BASE, shared, rest)
        bound = jnp.where(slot < BASE, even, jnp.where(slot < SEND - 1, count, 0))
        hot = ((rank == target) & (target < bound)).astype(f32).astype(bf16)
        picked = jnp.dot(hot, rows, preferred_element_type=f32)
        out_ref[q] = jnp.where(srow == SEND - 1, info, picked).astype(bf16)


def shares(counts, q):
    parts, start, offset = [], jnp.zeros_like(counts[0]), jnp.zeros_like(counts[0])
    for n in counts:
        rem = n & 7
        extra = (q - offset) & 7
        length = (n >> 3) + (extra < rem).astype(i32)
        parts.append((start, length, n >> 3, extra))
        start, offset = start + length, offset + rem
    return parts


def share_kernel(got_ref, out_ref):
    rep, own = lax.axis_index("rep"), lax.axis_index("b")
    q = 2 * rep + own
    counts = [
        got_ref[l, 0, SEND - 1 : SEND, T : 2 * T].astype(f32).astype(i32) for l in range(LAYERS)
    ]
    s = iota((SHARE, SEND), 0)
    slot = iota((SHARE, SEND), 1)
    total = [jnp.zeros((SHARE, KD), f32) for _ in range(2)]
    for l, (start, length, base, extra) in enumerate(shares(counts, q)):
        start, length, base, extra = (v[:, :SEND] for v in (start, length, base, extra))
        i = s - start
        inside = (i >= 0) & (i < length)
        want = jnp.where(i < base, i, BASE + extra)
        hot = (inside & (slot == want)).astype(f32).astype(bf16)
        for h in range(2):
            half = own if h == 0 else 1 - own
            total[h] += jnp.dot(hot, got_ref[l, half], preferred_element_type=f32)
    row = iota((SHARE, T), 0)
    info = jnp.zeros((SHARE, T), f32)
    for l in range(LAYERS):
        mine = got_ref[l, 0, SEND - 1 : SEND, :T].astype(f32)
        info = jnp.where((row == 0) & (rep == l), mine, info)
        info = jnp.where(row == 1 + l, counts[l].astype(f32), info)
    for z in range(Z):
        for h in range(2):
            out_ref[z, :, h * KD : (h + 1) * KD] = total[h].astype(bf16)
        out_ref[z, :, 2 * KD :] = info.astype(bf16)


def ladder_kernel(got_ref, *refs):
    pieces, out_ref, buffers, spread_ref, sems = refs[:4], refs[4], refs[5:9], refs[9], refs[10]
    copies = [pltpu.make_async_copy(pieces[n], buffers[n], sems.at[n]) for n in range(4)]
    for copy in copies:
        copy.start()
    q = 2 * lax.axis_index("rep") + lax.axis_index("b")
    own = lax.axis_index("k")
    lane = iota((1, Z * SHARE), 1)
    counts = []
    for l in range(LAYERS):
        n = jnp.zeros((1, Z * SHARE), f32)
        for z in range(Z):
            one = got_ref[z, 1 + l : 2 + l, 2 * KD :].astype(f32)
            n = jnp.where((lane >> 5) == z, jnp.concatenate([one, one], axis=1), n)
        counts.append(n.astype(i32))
    row = iota((ROWS, Z * SHARE), 0)
    col = iota((ROWS, Z * SHARE), 1)
    i = row & (BASE - 1)
    same = (row >> 4) == (col >> 5)
    rows = jnp.concatenate([got_ref[z, :, : 2 * KD] for z in range(Z)], axis=0)
    for l, (start, length, _, _) in enumerate(shares(counts, q)):
        hot = (same & (i < length) & ((col & (SHARE - 1)) == start + i)).astype(f32).astype(bf16)
        spread_ref[l * ROWS : (l + 1) * ROWS, :] = jnp.dot(
            hot, rows, preferred_element_type=f32
        ).astype(bf16)
    dims = (((1,), (1,)), ((), ()))
    for copy in copies:
        copy.wait()
    step = 256
    for side in range(2):
        for at in range(0, 512, step):
            part = jnp.zeros((step, LAYERS * ROWS), f32)
            for h in range(2):
                part += lax.dot_general(
                    buffers[2 * side + h][at : at + step, :],
                    spread_ref[:, h * KD : (h + 1) * KD],
                    dims,
                    preferred_element_type=f32,
                )
            core = own if side == 0 else 1 - own
            for l in range(LAYERS):
                out_ref[l, core, at : at + step, :] = part[:, l * ROWS : (l + 1) * ROWS]


def place_kernel(info_ref, out_ref):
    rep, own = lax.axis_index("rep"), lax.axis_index("k")

    def of(r):
        at_core = [
            jnp.concatenate([info_ref[s, z, r : r + 1, :].astype(f32) for z in range(Z)], axis=0)
            for s in range(2)
        ]
        first = jnp.where(own == 0, at_core[0], at_core[1])
        second = jnp.where(own == 0, at_core[1], at_core[0])
        return jnp.concatenate([first, second], axis=0)

    active = of(0)
    rank = ranks(active)
    offset = jnp.zeros((2 * Z, T), i32)
    even = jnp.zeros((2 * Z, T), i32)
    for l in range(LAYERS):
        n = of(1 + l).astype(i32)
        offset += jnp.where(l < rep, n & 7, 0)
        even = jnp.where(l == rep, (n >> 3) << 3, even)
    cls = jnp.where(rank < even, rank, offset + rank - even) & 7
    out_ref[0] = jnp.where(active > 0, cls, -1)
    out_ref[1] = jnp.minimum(rank >> 3, BASE - 1)


def final_kernel(place_ref, sums_ref, residual_ref, out_ref):
    for z in range(Z):
        for k in range(2):
            j = k * Z + z
            own = jnp.broadcast_to(place_ref[0, j : j + 1, :], (64, T))
            lane = BASE * z + jnp.broadcast_to(place_ref[1, j : j + 1, :], (64, T))
            ladder = jnp.zeros((64, T), f32)
            for q in range(CLASSES):
                here = jnp.take_along_axis(sums_ref[q // 2, k, q % 2], lane, axis=1)
                ladder = jnp.where(own == q, here, ladder)
            at = (z * 2 + k) * T
            old = residual_ref[:, at : at + T].astype(f32)
            out_ref[:, at : at + T] = (old + ladder).astype(bf16)


VMEM = pl.BlockSpec(memory_space=pltpu.VMEM)
ANY = pl.BlockSpec(memory_space=pl.ANY)
MIB = 2**20


def call(kernel, shape, dtype, *args, anys=0, scratch=(), limit=8, flops=0):
    return pl.pallas_call(
        kernel,
        out_shape=jax.ShapeDtypeStruct(shape, dtype),
        in_specs=[VMEM] * (len(args) - anys) + [ANY] * anys,
        out_specs=VMEM,
        scratch_shapes=scratch,
        compiler_params=pltpu.CompilerParams(vmem_limit_bytes=limit * MIB),
        cost_estimate=pl.CostEstimate(flops=flops, bytes_accessed=2**21, transcendentals=0),
    )(*args)


def step(amplitudes, pair_irrep, integrals, residual_in):
    swap = [(0, 1), (1, 0)]

    packed = call(pack_kernel, (CLASSES, SEND, KD), bf16, pair_irrep, amplitudes[0], flops=2**26)
    got = lax.all_to_all(packed, ("rep", "b"), 0, 0, tiled=True)
    got = got.reshape(LAYERS, 2, SEND, KD)
    shared = call(share_kernel, (Z, SHARE, 2 * KD + T), bf16, got, flops=2**26)
    gathered = lax.all_to_all(shared, "z", 0, 0, tiled=True)

    other = lax.ppermute(integrals, "b", swap)
    across = lax.ppermute(integrals, "k", swap)
    across_other = lax.ppermute(other, "k", swap)

    tall = pltpu.VMEM((512, KD), bf16)
    partial = call(
        ladder_kernel,
        (LAYERS, 2, 512, ROWS),
        f32,
        gathered,
        integrals,
        other,
        across,
        across_other,
        anys=4,
        scratch=[tall] * 4
        + [pltpu.VMEM((LAYERS * ROWS, 2 * KD), bf16), pltpu.SemaphoreType.DMA((4,))],
        limit=24,
        flops=2**31,
    )

    sent = partial.astype(jnp.float16).reshape(64, 64, ROWS)
    parts = lax.all_to_all(sent, ("rep", "k", "g", "b"), 0, 0, tiled=True)
    sums = jnp.sum(parts.reshape(LAYERS, 2, 4, 2, 64, ROWS).astype(f32), axis=2)

    info = gathered[:, :8, 2 * KD :]
    info_across = lax.ppermute(info, "k", swap)
    place = call(place_kernel, (2, 2 * Z, T), i32, jnp.stack([info, info_across]), flops=2**20)
    out = call(final_kernel, (64, 2048), bf16, place, sums, residual_in[0].T, flops=2**26)
    return out.T[None]


def solution(mesh):
    devices = mesh.devices.reshape(8, 2, 4, 2, 4)
    split = Mesh(devices, ("z", "k", "g", "b", "rep"))
    ab, cd = ("z", "k"), ("g", "b")
    return jax.shard_map(
        step,
        mesh=split,
        in_specs=(P("rep", ab, cd), P("rep", ab), P(ab, cd), P("rep", None, ab + cd)),
        out_specs=P("rep", None, ab + cd),
        check_vma=False,
    )
```

```python
import jax
import jax.numpy as jnp
from jax import lax
from jax.experimental import pallas as pl
from jax.experimental.pallas import tpu as pltpu
from jax.sharding import Mesh, PartitionSpec as P


LAYERS = 4
T = 128
KD = 1024
CLASSES = 8
BASE = 16
REST = 2 * BASE
SEND = REST + 8
SHARE = 32
Z = 8
ROWS = Z * BASE
i32, f32, bf16 = jnp.int32, jnp.float32, jnp.bfloat16


def iota(shape, dim):
    return lax.broadcasted_iota(i32, shape, dim)


def ranks(active):
    before = (iota((T, T), 0) < iota((T, T), 1)).astype(bf16)
    return jnp.dot(active.astype(bf16), before, preferred_element_type=f32).astype(i32)


def pack_kernel(labels_far, rows_far, out_ref, labels_ref, rows_ref, sems):
    labels_in = pltpu.make_async_copy(labels_far, labels_ref, sems.at[0])
    rows_in = pltpu.make_async_copy(rows_far, rows_ref, sems.at[1])
    labels_in.start()
    rows_in.start()
    labels_in.wait()
    active = jnp.broadcast_to(labels_ref[...] == 0, (8, T)).astype(i32).astype(f32)
    rank = jnp.where(active[:1] > 0, ranks(active)[:1], -1)
    count = jnp.sum(active, axis=1, keepdims=True).astype(i32)[:1]
    even = (count >> 3) << 3
    rows_in.wait()
    rows = rows_ref[...]
    slot = iota((SEND, T), 0)
    lane = iota((SEND, KD), 1)
    srow = iota((SEND, KD), 0)
    flags = jnp.concatenate([active[:1]] * (KD // T), axis=1)
    info = jnp.where(lane < T, flags, count.astype(f32))
    for rep in range(LAYERS):
        shared = 8 * (slot & (BASE - 1)) + 2 * rep + (slot >> 4)
        rest = even + slot - REST
        target = jnp.where(slot < REST, shared, rest)
        bound = jnp.where(slot < REST, even, jnp.where(slot < SEND - 1, count, 0))
        hot = ((rank == target) & (target < bound)).astype(f32).astype(bf16)
        picked = jnp.dot(hot, rows, preferred_element_type=f32)
        out_ref[rep] = jnp.where(srow == SEND - 1, info, picked).astype(bf16)


def shares(counts, q):
    parts, start, offset = [], jnp.zeros_like(counts[0]), jnp.zeros_like(counts[0])
    for n in counts:
        rem = n & 7
        extra = (q - offset) & 7
        length = (n >> 3) + (extra < rem).astype(i32)
        parts.append((start, length, n >> 3, extra))
        start, offset = start + length, offset + rem
    return parts


def share_kernel(got_ref, out_ref):
    rep = lax.axis_index("rep")
    counts = [got_ref[l, SEND - 1 : SEND, T : 2 * T].astype(f32).astype(i32) for l in range(LAYERS)]
    row = iota((SHARE, T), 0)
    info = jnp.zeros((SHARE, T), f32)
    for l in range(LAYERS):
        mine = got_ref[l, SEND - 1 : SEND, :T].astype(f32)
        info = jnp.where((row == 0) & (rep == l), mine, info)
        info = jnp.where(row == 1 + l, counts[l].astype(f32), info)
    s = iota((SHARE, SEND), 0)
    slot = iota((SHARE, SEND), 1)
    for b in range(2):
        total = jnp.zeros((SHARE, KD), f32)
        for l, parts in enumerate(shares(counts, 2 * rep + b)):
            start, length, base, extra = (v[:, :SEND] for v in parts)
            i = s - start
            inside = (i >= 0) & (i < length)
            want = jnp.where(i < base, BASE * b + i, REST + extra)
            hot = (inside & (slot == want)).astype(f32).astype(bf16)
            total += jnp.dot(hot, got_ref[l], preferred_element_type=f32)
        for z in range(Z):
            out_ref[b, z, :, :KD] = total.astype(bf16)
            out_ref[b, z, :, KD:] = info.astype(bf16)


def ladder_kernel(got_ref, *refs):
    pieces, out_ref, buffers, spread_ref, sems = refs[:4], refs[4], refs[5:9], refs[9], refs[10]
    copies = [pltpu.make_async_copy(pieces[n], buffers[n], sems.at[n]) for n in range(4)]
    for copy in copies:
        copy.start()
    q = 2 * lax.axis_index("rep") + lax.axis_index("b")
    own = lax.axis_index("k")
    lane = iota((1, Z * SHARE), 1)
    counts = []
    for l in range(LAYERS):
        n = jnp.zeros((1, Z * SHARE), f32)
        for z in range(Z):
            one = got_ref[0, z, 1 + l : 2 + l, KD:].astype(f32)
            n = jnp.where((lane >> 5) == z, jnp.concatenate([one, one], axis=1), n)
        counts.append(n.astype(i32))
    row = iota((ROWS, Z * SHARE), 0)
    col = iota((ROWS, Z * SHARE), 1)
    i = row & (BASE - 1)
    same = (row >> 4) == (col >> 5)
    pair = lax.axis_index("b")
    rows = jnp.concatenate(
        [
            jnp.concatenate([got_ref[half, z, :, :KD] for z in range(Z)], axis=0)
            for half in (pair, 1 - pair)
        ],
        axis=1,
    )
    for l, (start, length, _, _) in enumerate(shares(counts, q)):
        hot = (same & (i < length) & ((col & (SHARE - 1)) == start + i)).astype(f32).astype(bf16)
        spread_ref[l * ROWS : (l + 1) * ROWS, :] = jnp.dot(
            hot, rows, preferred_element_type=f32
        ).astype(bf16)
    dims = (((1,), (1,)), ((), ()))
    for copy in copies:
        copy.wait()
    step = 256
    for side in range(2):
        for at in range(0, 512, step):
            part = jnp.zeros((step, LAYERS * ROWS), f32)
            for h in range(2):
                part += lax.dot_general(
                    buffers[2 * side + h][at : at + step, :],
                    spread_ref[:, h * KD : (h + 1) * KD],
                    dims,
                    preferred_element_type=f32,
                )
            core = own if side == 0 else 1 - own
            for l in range(LAYERS):
                out_ref[l, core, at : at + step, :] = part[:, l * ROWS : (l + 1) * ROWS]


def place_kernel(info_ref, out_ref):
    rep, own = lax.axis_index("rep"), lax.axis_index("k")

    def of(r):
        at_core = [
            jnp.concatenate([info_ref[s, z, r : r + 1, :].astype(f32) for z in range(Z)], axis=0)
            for s in range(2)
        ]
        first = jnp.where(own == 0, at_core[0], at_core[1])
        second = jnp.where(own == 0, at_core[1], at_core[0])
        return jnp.concatenate([first, second], axis=0)

    active = of(0)
    rank = ranks(active)
    offset = jnp.zeros((2 * Z, T), i32)
    even = jnp.zeros((2 * Z, T), i32)
    for l in range(LAYERS):
        n = of(1 + l).astype(i32)
        offset += jnp.where(l < rep, n & 7, 0)
        even = jnp.where(l == rep, (n >> 3) << 3, even)
    cls = jnp.where(rank < even, rank, offset + rank - even) & 7
    out_ref[0] = jnp.where(active > 0, cls, -1)
    out_ref[1] = jnp.minimum(rank >> 3, BASE - 1)


def final_kernel(place_ref, sums_ref, residual_ref, out_ref):
    for z in range(Z):
        for k in range(2):
            j = k * Z + z
            own = jnp.broadcast_to(place_ref[0, j : j + 1, :], (64, T))
            lane = BASE * z + jnp.broadcast_to(place_ref[1, j : j + 1, :], (64, T))
            ladder = jnp.zeros((64, T), f32)
            for q in range(CLASSES):
                here = jnp.take_along_axis(sums_ref[q // 2, k, q % 2], lane, axis=1)
                ladder = jnp.where(own == q, here, ladder)
            at = (z * 2 + k) * T
            old = residual_ref[:, at : at + T].astype(f32)
            out_ref[:, at : at + T] = (old + ladder).astype(bf16)


VMEM = pl.BlockSpec(memory_space=pltpu.VMEM)
HBM = pl.BlockSpec(memory_space=pltpu.HBM)
MIB = 2**20


def call(kernel, shape, dtype, *args, far=0, scratch=(), limit=8, flops=0):
    return pl.pallas_call(
        kernel,
        out_shape=jax.ShapeDtypeStruct(shape, dtype),
        in_specs=[VMEM] * (len(args) - far) + [HBM] * far,
        out_specs=VMEM,
        scratch_shapes=scratch,
        compiler_params=pltpu.CompilerParams(vmem_limit_bytes=limit * MIB),
        cost_estimate=pl.CostEstimate(flops=flops, bytes_accessed=2**21, transcendentals=0),
    )(*args)


def step(amplitudes, pair_irrep, integrals, residual_in):
    swap = [(0, 1), (1, 0)]

    packed = call(
        pack_kernel,
        (LAYERS, SEND, KD),
        bf16,
        pair_irrep,
        amplitudes[0],
        far=2,
        scratch=[pltpu.VMEM((1, T), i32), pltpu.VMEM((T, KD), bf16), pltpu.SemaphoreType.DMA((2,))],
        flops=2**26,
    )
    got = lax.all_to_all(packed, "rep", 0, 0, tiled=True)
    shared = call(share_kernel, (2, Z, SHARE, KD + T), bf16, got, flops=2**26)
    gathered = lax.all_to_all(
        shared.reshape(2 * Z, SHARE, KD + T), ("b", "z"), 0, 0, tiled=True
    ).reshape(2, Z, SHARE, KD + T)

    other = lax.ppermute(integrals, "b", swap)
    across = lax.ppermute(integrals, "k", swap)
    across_other = lax.ppermute(other, "k", swap)

    tall = pltpu.VMEM((512, KD), bf16)
    partial = call(
        ladder_kernel,
        (LAYERS, 2, 512, ROWS),
        f32,
        gathered,
        integrals,
        other,
        across,
        across_other,
        far=4,
        scratch=[tall] * 4
        + [pltpu.VMEM((LAYERS * ROWS, 2 * KD), bf16), pltpu.SemaphoreType.DMA((4,))],
        limit=54,
        flops=2**31,
    )

    sent = partial.astype(jnp.float16).reshape(64, 64, ROWS)
    parts = lax.all_to_all(sent, ("rep", "k", "g", "b"), 0, 0, tiled=True)
    sums = jnp.sum(parts.reshape(LAYERS, 2, 4, 2, 64, ROWS).astype(f32), axis=2)

    info = gathered[0, :, :8, KD:]
    info_across = lax.ppermute(info, "k", swap)
    place = call(place_kernel, (2, 2 * Z, T), i32, jnp.stack([info, info_across]), flops=2**20)
    out = call(final_kernel, (64, 2048), bf16, place, sums, residual_in[0].T, flops=2**26)
    return out.T[None]


def solution(mesh):
    devices = mesh.devices.reshape(8, 2, 4, 2, 4)
    split = Mesh(devices, ("z", "k", "g", "b", "rep"))
    ab, cd = ("z", "k"), ("g", "b")
    return jax.shard_map(
        step,
        mesh=split,
        in_specs=(P("rep", ab, cd), P("rep", ab), P(ab, cd), P("rep", None, ab + cd)),
        out_specs=P("rep", None, ab + cd),
        check_vma=False,
    )
```

```python
import jax
import jax.numpy as jnp
from jax import lax
from jax.experimental import pallas as pl
from jax.experimental.pallas import tpu as pltpu
from jax.sharding import Mesh, PartitionSpec as P


LAYERS = 4
T = 128
KD = 1024
CLASSES = 8
BASE = 16
REST = 2 * BASE
SEND = REST + 8
SHARE = 32
Z = 8
i32, f32, bf16 = jnp.int32, jnp.float32, jnp.bfloat16


def iota(shape, dim):
    return lax.broadcasted_iota(i32, shape, dim)


def ranks(active):
    before = (iota((T, T), 0) < iota((T, T), 1)).astype(bf16)
    return jnp.dot(active.astype(bf16), before, preferred_element_type=f32).astype(i32)


def pack_kernel(labels_ref, rows_ref, out_ref):
    active = jnp.broadcast_to(labels_ref[...] == 0, (8, T)).astype(i32).astype(f32)
    rank = jnp.where(active[:1] > 0, ranks(active)[:1], -1)
    count = jnp.sum(active, axis=1, keepdims=True).astype(i32)[:1]
    even = (count >> 3) << 3
    rows = rows_ref[...]
    slot = iota((SEND, T), 0)
    lane = iota((SEND, KD), 1)
    srow = iota((SEND, KD), 0)
    flags = jnp.concatenate([active[:1]] * (KD // T), axis=1)
    info = jnp.where(lane < T, flags, count.astype(f32))
    for rep in range(LAYERS):
        shared = 8 * (slot & (BASE - 1)) + 2 * rep + (slot >> 4)
        rest = even + slot - REST
        target = jnp.where(slot < REST, shared, rest)
        bound = jnp.where(slot < REST, even, jnp.where(slot < SEND - 1, count, 0))
        hot = ((rank == target) & (target < bound)).astype(f32).astype(bf16)
        picked = jnp.dot(hot, rows, preferred_element_type=f32)
        out_ref[rep] = jnp.where(srow == SEND - 1, info, picked).astype(bf16)


def shares(counts, q):
    parts, start, offset = [], jnp.zeros_like(counts[0]), jnp.zeros_like(counts[0])
    for n in counts:
        rem = n & 7
        extra = (q - offset) & 7
        length = (n >> 3) + (extra < rem).astype(i32)
        parts.append((start, length, n >> 3, extra))
        start, offset = start + length, offset + rem
    return parts


def share_kernel(got_ref, out_ref):
    rep = lax.axis_index("rep")
    counts = [got_ref[l, SEND - 1 : SEND, T : 2 * T].astype(f32).astype(i32) for l in range(LAYERS)]
    row = iota((SHARE, T), 0)
    info = jnp.zeros((SHARE, T), f32)
    for l in range(LAYERS):
        mine = got_ref[l, SEND - 1 : SEND, :T].astype(f32)
        info = jnp.where((row == 0) & (rep == l), mine, info)
        info = jnp.where(row == 1 + l, counts[l].astype(f32), info)
    s = iota((SHARE, SEND), 0)
    slot = iota((SHARE, SEND), 1)
    for b in range(2):
        total = jnp.zeros((SHARE, KD), f32)
        for l, parts in enumerate(shares(counts, 2 * rep + b)):
            start, length, base, extra = (v[:, :SEND] for v in parts)
            i = s - start
            inside = (i >= 0) & (i < length)
            want = jnp.where(i < base, BASE * b + i, REST + extra)
            hot = (inside & (slot == want)).astype(f32).astype(bf16)
            total += jnp.dot(hot, got_ref[l], preferred_element_type=f32)
        for z in range(Z):
            out_ref[b, z, :, :KD] = total.astype(bf16)
            out_ref[b, z, :, KD:] = info.astype(bf16)


def ladder_kernel(got_ref, *refs):
    pieces, out_ref, buffers, sems = refs[:4], refs[4], refs[5:9], refs[9]
    copies = [pltpu.make_async_copy(pieces[n], buffers[n], sems.at[n]) for n in range(4)]
    for copy in copies:
        copy.start()
    own, pair = lax.axis_index("k"), lax.axis_index("b")
    rows = [
        jnp.concatenate([got_ref[half, z, :, :KD] for z in range(Z)], axis=0)
        for half in (pair, 1 - pair)
    ]
    dims = (((1,), (1,)), ((), ()))
    for side in range(2):
        part = jnp.zeros((512, Z * SHARE), f32)
        for h in range(2):
            copies[2 * side + h].wait()
            part += lax.dot_general(
                buffers[2 * side + h][...], rows[h], dims, preferred_element_type=f32
            )
        out_ref[own if side == 0 else 1 - own] = part


def plan_kernel(info_ref, place_ref, route_ref):
    rep, own = lax.axis_index("rep"), lax.axis_index("k")

    def of(r):
        at_core = [
            jnp.concatenate([info_ref[s, z, r : r + 1, :].astype(f32) for z in range(Z)], axis=0)
            for s in range(2)
        ]
        first = jnp.where(own == 0, at_core[0], at_core[1])
        second = jnp.where(own == 0, at_core[1], at_core[0])
        return jnp.concatenate([first, second], axis=0)

    active = of(0)
    rank = ranks(active)
    offset = jnp.zeros((2 * Z, T), i32)
    even = jnp.zeros((2 * Z, T), i32)
    counts = [of(1 + l).astype(i32) for l in range(LAYERS)]
    for l, n in enumerate(counts):
        offset += jnp.where(l < rep, n & 7, 0)
        even = jnp.where(l == rep, (n >> 3) << 3, even)
    cls = jnp.where(rank < even, rank, offset + rank - even) & 7
    place_ref[0] = jnp.where(active > 0, cls, -1)
    place_ref[1] = jnp.minimum(rank >> 3, BASE - 1)

    lane = iota((1, T), 1)
    for k in range(2):
        spread = []
        for n in counts:
            at = jnp.zeros((1, T), i32)
            for z in range(Z):
                at = jnp.where((lane >> 4) == z, n[k * Z + z : k * Z + z + 1], at)
            spread.append(at)
        for b in range(2):
            for l, (start, _, _, _) in enumerate(shares(spread, 2 * rep + b)):
                source = SHARE * ((lane >> 4) & 3) + start + (lane & (BASE - 1))
                route_ref[(l * 2 + k) * 2 + b : (l * 2 + k) * 2 + b + 1, :] = source & (T - 1)


def route_kernel(route_ref, sums_ref, out_ref):
    low = iota((64, T), 1) < T // 2
    for k in range(2):
        for b in range(2):
            halves = [sums_ref[k, b, :, h * T : (h + 1) * T] for h in range(2)]
            for l in range(LAYERS):
                row = (l * 2 + k) * 2 + b
                source = jnp.broadcast_to(route_ref[row : row + 1, :], (64, T))
                first, second = (jnp.take_along_axis(x, source, axis=1) for x in halves)
                out_ref[l, k, b] = jnp.where(low, first, second)


def final_kernel(place_ref, sums_ref, residual_ref, out_ref):
    for z in range(Z):
        for k in range(2):
            j = k * Z + z
            own = jnp.broadcast_to(place_ref[0, j : j + 1, :], (64, T))
            lane = BASE * z + jnp.broadcast_to(place_ref[1, j : j + 1, :], (64, T))
            ladder = jnp.zeros((64, T), f32)
            for q in range(CLASSES):
                here = jnp.take_along_axis(sums_ref[q // 2, k, q % 2], lane, axis=1)
                ladder = jnp.where(own == q, here, ladder)
            at = (z * 2 + k) * T
            old = residual_ref[:, at : at + T].astype(f32)
            out_ref[:, at : at + T] = (old + ladder).astype(bf16)


VMEM = pl.BlockSpec(memory_space=pltpu.VMEM)
HBM = pl.BlockSpec(memory_space=pltpu.HBM)
MIB = 2**20


def call(kernel, shape, dtype, *args, far=0, scratch=(), limit=8, flops=0):
    return pl.pallas_call(
        kernel,
        out_shape=[jax.ShapeDtypeStruct(one, dtype) for one in shape]
        if isinstance(shape, list)
        else jax.ShapeDtypeStruct(shape, dtype),
        in_specs=[VMEM] * (len(args) - far) + [HBM] * far,
        out_specs=[VMEM] * len(shape) if isinstance(shape, list) else VMEM,
        scratch_shapes=scratch,
        compiler_params=pltpu.CompilerParams(vmem_limit_bytes=limit * MIB),
        cost_estimate=pl.CostEstimate(flops=flops, bytes_accessed=2**21, transcendentals=0),
    )(*args)


def step(amplitudes, pair_irrep, integrals, residual_in):
    swap = [(0, 1), (1, 0)]

    packed = call(pack_kernel, (LAYERS, SEND, KD), bf16, pair_irrep, amplitudes[0], flops=2**26)
    got = lax.all_to_all(packed, "rep", 0, 0, tiled=True)
    shared = call(share_kernel, (2, Z, SHARE, KD + T), bf16, got, flops=2**26)
    gathered = lax.all_to_all(
        shared.reshape(2 * Z, SHARE, KD + T), ("b", "z"), 0, 0, tiled=True
    ).reshape(2, Z, SHARE, KD + T)

    other = lax.ppermute(integrals, "b", swap)
    across = lax.ppermute(integrals, "k", swap)
    across_other = lax.ppermute(other, "k", swap)

    partial = call(
        ladder_kernel,
        (2, 512, Z * SHARE),
        f32,
        gathered,
        integrals,
        other,
        across,
        across_other,
        far=4,
        scratch=[pltpu.VMEM((512, KD), bf16)] * 4 + [pltpu.SemaphoreType.DMA((4,))],
        limit=48,
        flops=2**30,
    )

    sent = partial.astype(jnp.float16).reshape(16, 64, Z * SHARE)
    parts = lax.all_to_all(sent, ("k", "g", "b"), 0, 0, tiled=True)
    sums = jnp.sum(parts.reshape(2, 4, 2, 64, Z * SHARE).astype(f32), axis=1)

    info = gathered[0, :, :8, KD:]
    info_across = lax.ppermute(info, "k", swap)
    place, route = call(
        plan_kernel, [(2, 2 * Z, T), (16, T)], i32, jnp.stack([info, info_across]), flops=2**20
    )
    routed = call(route_kernel, (LAYERS, 2, 2, 64, T), f32, route, sums, flops=2**24)
    owned = lax.all_to_all(routed, "rep", 0, 0, tiled=True)
    out = call(final_kernel, (64, 2048), bf16, place, owned, residual_in[0].T, flops=2**26)
    return out.T[None]


def solution(mesh):
    devices = mesh.devices.reshape(8, 2, 4, 2, 4)
    split = Mesh(devices, ("z", "k", "g", "b", "rep"))
    ab, cd = ("z", "k"), ("g", "b")
    return jax.shard_map(
        step,
        mesh=split,
        in_specs=(P("rep", ab, cd), P("rep", ab), P(ab, cd), P("rep", None, ab + cd)),
        out_specs=P("rep", None, ab + cd),
        check_vma=False,
    )
```

```python
import jax
import jax.numpy as jnp
from jax import lax
from jax.experimental import pallas as pl
from jax.experimental.pallas import tpu as pltpu
from jax.sharding import Mesh, PartitionSpec as P


LAYERS = 4
T = 128
KD = 1024
CLASSES = 8
BASE = 16
REST = 2 * BASE
SEND = REST + 8
SHARE = 32
Z = 8
i32, f32, bf16 = jnp.int32, jnp.float32, jnp.bfloat16


def iota(shape, dim):
    return lax.broadcasted_iota(i32, shape, dim)


def ranks(active):
    before = (iota((T, T), 0) < iota((T, T), 1)).astype(bf16)
    return jnp.dot(active.astype(bf16), before, preferred_element_type=f32).astype(i32)


def pack_kernel(labels_ref, rows_ref, out_ref):
    active = jnp.broadcast_to(labels_ref[...] == 0, (8, T)).astype(i32).astype(f32)
    rank = jnp.where(active[:1] > 0, ranks(active)[:1], -1)
    count = jnp.sum(active, axis=1, keepdims=True).astype(i32)[:1]
    even = (count >> 3) << 3
    rows = rows_ref[...]
    slot = iota((SEND, T), 0)
    lane = iota((SEND, KD), 1)
    srow = iota((SEND, KD), 0)
    flags = jnp.concatenate([active[:1]] * (KD // T), axis=1)
    info = jnp.where(lane < T, flags, count.astype(f32))
    for rep in range(LAYERS):
        shared = 8 * (slot & (BASE - 1)) + 2 * rep + (slot >> 4)
        rest = even + slot - REST
        target = jnp.where(slot < REST, shared, rest)
        bound = jnp.where(slot < REST, even, jnp.where(slot < SEND - 1, count, 0))
        hot = ((rank == target) & (target < bound)).astype(f32).astype(bf16)
        picked = jnp.dot(hot, rows, preferred_element_type=f32)
        out_ref[rep] = jnp.where(srow == SEND - 1, info, picked).astype(bf16)


def shares(counts, q):
    parts, start, offset = [], jnp.zeros_like(counts[0]), jnp.zeros_like(counts[0])
    for n in counts:
        rem = n & 7
        extra = (q - offset) & 7
        length = (n >> 3) + (extra < rem).astype(i32)
        parts.append((start, length, n >> 3, extra))
        start, offset = start + length, offset + rem
    return parts


def share_kernel(got_ref, out_ref):
    rep = lax.axis_index("rep")
    counts = [got_ref[l, SEND - 1 : SEND, T : 2 * T].astype(f32).astype(i32) for l in range(LAYERS)]
    row = iota((SHARE, T), 0)
    info = jnp.zeros((SHARE, T), f32)
    for l in range(LAYERS):
        mine = got_ref[l, SEND - 1 : SEND, :T].astype(f32)
        info = jnp.where((row == 0) & (rep == l), mine, info)
        info = jnp.where(row == 1 + l, counts[l].astype(f32), info)
    s = iota((SHARE, SEND), 0)
    slot = iota((SHARE, SEND), 1)
    for b in range(2):
        total = jnp.zeros((SHARE, KD), f32)
        for l, parts in enumerate(shares(counts, 2 * rep + b)):
            start, length, base, extra = (v[:, :SEND] for v in parts)
            i = s - start
            inside = (i >= 0) & (i < length)
            want = jnp.where(i < base, BASE * b + i, REST + extra)
            hot = (inside & (slot == want)).astype(f32).astype(bf16)
            total += jnp.dot(hot, got_ref[l], preferred_element_type=f32)
        for z in range(Z):
            out_ref[b, z, :, :KD] = total.astype(bf16)
            out_ref[b, z, :, KD:] = info.astype(bf16)


def ladder_kernel(own_ref, pair_ref, got_far, across_far, across_pair_far, out_ref, *scratch):
    got_ref, across_ref, across_pair_ref, sems = scratch
    far = ((got_far, got_ref), (across_far, across_ref), (across_pair_far, across_pair_ref))
    copies = [pltpu.make_async_copy(*two, sems.at[n]) for n, two in enumerate(far)]
    for copy in copies:
        copy.start()
    own, pair = lax.axis_index("k"), lax.axis_index("b")
    dims = (((1,), (1,)), ((), ()))
    copies[0].wait()
    rows = [
        jnp.concatenate([got_ref[half, z, :, :KD] for z in range(Z)], axis=0)
        for half in (pair, 1 - pair)
    ]

    def part(piece, half):
        return lax.dot_general(piece[...], half, dims, preferred_element_type=f32)

    out_ref[own] = part(own_ref, rows[0]) + part(pair_ref, rows[1])
    copies[1].wait()
    copies[2].wait()
    out_ref[1 - own] = part(across_ref, rows[0]) + part(across_pair_ref, rows[1])


def plan_kernel(info_ref, place_ref, route_ref):
    rep, own = lax.axis_index("rep"), lax.axis_index("k")

    def of(r):
        at_core = [
            jnp.concatenate([info_ref[s, z, r : r + 1, :].astype(f32) for z in range(Z)], axis=0)
            for s in range(2)
        ]
        first = jnp.where(own == 0, at_core[0], at_core[1])
        second = jnp.where(own == 0, at_core[1], at_core[0])
        return jnp.concatenate([first, second], axis=0)

    active = of(0)
    rank = ranks(active)
    offset = jnp.zeros((2 * Z, T), i32)
    even = jnp.zeros((2 * Z, T), i32)
    counts = [of(1 + l).astype(i32) for l in range(LAYERS)]
    for l, n in enumerate(counts):
        offset += jnp.where(l < rep, n & 7, 0)
        even = jnp.where(l == rep, (n >> 3) << 3, even)
    cls = jnp.where(rank < even, rank, offset + rank - even) & 7
    place_ref[0] = jnp.where(active > 0, cls, -1)
    place_ref[1] = jnp.minimum(rank >> 3, BASE - 1)

    lane = iota((1, T), 1)
    for k in range(2):
        spread = []
        for n in counts:
            at = jnp.zeros((1, T), i32)
            for z in range(Z):
                at = jnp.where((lane >> 4) == z, n[k * Z + z : k * Z + z + 1], at)
            spread.append(at)
        for b in range(2):
            for l, (start, _, _, _) in enumerate(shares(spread, 2 * rep + b)):
                source = SHARE * ((lane >> 4) & 3) + start + (lane & (BASE - 1))
                route_ref[(l * 2 + k) * 2 + b : (l * 2 + k) * 2 + b + 1, :] = source & (T - 1)


def route_kernel(route_ref, sums_ref, out_ref):
    low = iota((64, T), 1) < T // 2
    for k in range(2):
        for b in range(2):
            halves = [sums_ref[k, b, :, h * T : (h + 1) * T] for h in range(2)]
            for l in range(LAYERS):
                row = (l * 2 + k) * 2 + b
                source = jnp.broadcast_to(route_ref[row : row + 1, :], (64, T))
                first, second = (jnp.take_along_axis(x, source, axis=1) for x in halves)
                out_ref[l, k, b] = jnp.where(low, first, second)


def final_kernel(place_ref, sums_ref, residual_ref, out_ref):
    for z in range(Z):
        for k in range(2):
            j = k * Z + z
            own = jnp.broadcast_to(place_ref[0, j : j + 1, :], (64, T))
            lane = BASE * z + jnp.broadcast_to(place_ref[1, j : j + 1, :], (64, T))
            ladder = jnp.zeros((64, T), f32)
            for q in range(CLASSES):
                here = jnp.take_along_axis(sums_ref[q // 2, k, q % 2], lane, axis=1)
                ladder = jnp.where(own == q, here, ladder)
            at = (z * 2 + k) * T
            old = residual_ref[:, at : at + T].astype(f32)
            out_ref[:, at : at + T] = (old + ladder).astype(bf16)


VMEM = pl.BlockSpec(memory_space=pltpu.VMEM)
HBM = pl.BlockSpec(memory_space=pltpu.HBM)
MIB = 2**20


def call(kernel, shape, dtype, *args, far=0, scratch=(), limit=8, flops=0):
    return pl.pallas_call(
        kernel,
        out_shape=[jax.ShapeDtypeStruct(one, dtype) for one in shape]
        if isinstance(shape, list)
        else jax.ShapeDtypeStruct(shape, dtype),
        in_specs=[VMEM] * (len(args) - far) + [HBM] * far,
        out_specs=[VMEM] * len(shape) if isinstance(shape, list) else VMEM,
        scratch_shapes=scratch,
        compiler_params=pltpu.CompilerParams(vmem_limit_bytes=limit and limit * MIB),
        cost_estimate=pl.CostEstimate(flops=flops, bytes_accessed=2**21, transcendentals=0),
    )(*args)


def step(amplitudes, pair_irrep, integrals, residual_in):
    swap = [(0, 1), (1, 0)]

    packed = call(pack_kernel, (LAYERS, SEND, KD), bf16, pair_irrep, amplitudes[0], limit=None, flops=2**26)
    got = lax.all_to_all(packed, "rep", 0, 0, tiled=True)
    shared = call(share_kernel, (2, Z, SHARE, KD + T), bf16, got, flops=2**26)
    gathered = lax.all_to_all(
        shared.reshape(2 * Z, SHARE, KD + T), ("b", "z"), 0, 0, tiled=True
    ).reshape(2, Z, SHARE, KD + T)

    other = lax.ppermute(integrals, "b", swap)
    across = lax.ppermute(integrals, "k", swap)
    across_other = lax.ppermute(other, "k", swap)

    partial = call(
        ladder_kernel,
        (2, 512, Z * SHARE),
        f32,
        integrals,
        other,
        gathered,
        across,
        across_other,
        far=3,
        scratch=[
            pltpu.VMEM((2, Z, SHARE, KD + T), bf16),
            pltpu.VMEM((512, KD), bf16),
            pltpu.VMEM((512, KD), bf16),
            pltpu.SemaphoreType.DMA((3,)),
        ],
        limit=49,
        flops=2**30,
    )

    sent = partial.astype(jnp.float16).reshape(16, 64, Z * SHARE)
    parts = lax.all_to_all(sent, ("k", "g", "b"), 0, 0, tiled=True)
    sums = jnp.sum(parts.reshape(2, 4, 2, 64, Z * SHARE).astype(f32), axis=1)

    info = gathered[0, :, :8, KD:]
    info_across = lax.ppermute(info, "k", swap)
    place, route = call(
        plan_kernel, [(2, 2 * Z, T), (16, T)], i32, jnp.stack([info, info_across]), flops=2**20
    )
    routed = call(route_kernel, (LAYERS, 2, 2, 64, T), f32, route, sums, flops=2**24)
    owned = lax.all_to_all(routed, "rep", 0, 0, tiled=True)
    out = call(final_kernel, (64, 2048), bf16, place, owned, residual_in[0].T, flops=2**26)
    return out.T[None]


def solution(mesh):
    devices = mesh.devices.reshape(8, 2, 4, 2, 4)
    split = Mesh(devices, ("z", "k", "g", "b", "rep"))
    ab, cd = ("z", "k"), ("g", "b")
    return jax.shard_map(
        step,
        mesh=split,
        in_specs=(P("rep", ab, cd), P("rep", ab), P(ab, cd), P("rep", None, ab + cd)),
        out_specs=P("rep", None, ab + cd),
        check_vma=False,
    )
```

```python
import jax
import jax.numpy as jnp
from jax import lax
from jax.experimental import pallas as pl
from jax.experimental.pallas import tpu as pltpu
from jax.sharding import Mesh, PartitionSpec as P


LAYERS = 4
T = 128
KD = 1024
CLASSES = 8
BASE = 16
REST = 2 * BASE
SEND = REST + 8
SHARE = 32
Z = 8
i32, f32, bf16 = jnp.int32, jnp.float32, jnp.bfloat16


def iota(shape, dim):
    return lax.broadcasted_iota(i32, shape, dim)


def ranks(active):
    before = (iota((T, T), 0) < iota((T, T), 1)).astype(bf16)
    return jnp.dot(active.astype(bf16), before, preferred_element_type=f32).astype(i32)


def pack_kernel(labels_ref, rows_ref, out_ref):
    active = jnp.broadcast_to(labels_ref[...] == 0, (8, T)).astype(i32).astype(f32)
    rank = jnp.where(active[:1] > 0, ranks(active)[:1], -1)
    count = jnp.sum(active, axis=1, keepdims=True).astype(i32)[:1]
    even = (count >> 3) << 3
    rows = rows_ref[...]
    slot = iota((SEND, T), 0)
    lane = iota((SEND, KD), 1)
    srow = iota((SEND, KD), 0)
    flags = jnp.concatenate([active[:1]] * (KD // T), axis=1)
    info = jnp.where(lane < T, flags, count.astype(f32))
    for rep in range(LAYERS):
        shared = 8 * (slot & (BASE - 1)) + 2 * rep + (slot >> 4)
        rest = even + slot - REST
        target = jnp.where(slot < REST, shared, rest)
        bound = jnp.where(slot < REST, even, jnp.where(slot < SEND - 1, count, 0))
        hot = ((rank == target) & (target < bound)).astype(f32).astype(bf16)
        picked = jnp.dot(hot, rows, preferred_element_type=f32)
        out_ref[rep] = jnp.where(srow == SEND - 1, info, picked).astype(bf16)


def shares(counts, q):
    parts, start, offset = [], jnp.zeros_like(counts[0]), jnp.zeros_like(counts[0])
    for n in counts:
        rem = n & 7
        extra = (q - offset) & 7
        length = (n >> 3) + (extra < rem).astype(i32)
        parts.append((start, length, n >> 3, extra))
        start, offset = start + length, offset + rem
    return parts


def share_kernel(got_ref, out_ref, info_ref):
    rep = lax.axis_index("rep")
    counts = [got_ref[l, SEND - 1 : SEND, T : 2 * T].astype(f32).astype(i32) for l in range(LAYERS)]
    row = iota((8, T), 0)
    info = jnp.zeros((8, T), f32)
    for l in range(LAYERS):
        mine = got_ref[l, SEND - 1 : SEND, :T].astype(f32)
        info = jnp.where((row == 0) & (rep == l), mine, info)
        info = jnp.where(row == 1 + l, counts[l].astype(f32), info)
    info_ref[0] = info.astype(bf16)
    s = iota((SHARE, SEND), 0)
    slot = iota((SHARE, SEND), 1)
    for b in range(2):
        total = jnp.zeros((SHARE, KD), f32)
        for l, parts in enumerate(shares(counts, 2 * rep + b)):
            start, length, base, extra = (v[:, :SEND] for v in parts)
            i = s - start
            inside = (i >= 0) & (i < length)
            want = jnp.where(i < base, BASE * b + i, REST + extra)
            hot = (inside & (slot == want)).astype(f32).astype(bf16)
            total += jnp.dot(hot, got_ref[l], preferred_element_type=f32)
        for z in range(Z):
            out_ref[b, z] = total.astype(bf16)


def ladder_kernel(own_ref, pair_ref, got_ref, across_far, across_pair_far, out_ref, *scratch):
    across_ref, across_pair_ref, sems = scratch
    own, pair = lax.axis_index("k"), lax.axis_index("b")
    moves = ((across_far, across_ref), (across_pair_far, across_pair_ref))
    copies = [pltpu.make_async_copy(*move, sems.at[n]) for n, move in enumerate(moves)]
    for copy in copies:
        copy.start()

    def part(piece, half):
        dims = (((1,), (1,)), ((), ()))
        return lax.dot_general(piece[...], got_ref[half], dims, preferred_element_type=f32)

    out_ref[own] = part(own_ref, pair) + part(pair_ref, 1 - pair)
    copies[0].wait()
    far = part(across_ref, pair)
    copies[1].wait()
    out_ref[1 - own] = far + part(across_pair_ref, 1 - pair)


def plan_kernel(info_ref, place_ref, route_ref):
    rep, own, here = lax.axis_index("rep"), lax.axis_index("k"), lax.axis_index("z")

    def of(r):
        entries = [here ^ z for z in range(Z)]
        at_core = [
            jnp.concatenate([info_ref[s, e, r : r + 1, :].astype(f32) for e in entries], axis=0)
            for s in range(2)
        ]
        first = jnp.where(own == 0, at_core[0], at_core[1])
        second = jnp.where(own == 0, at_core[1], at_core[0])
        return jnp.concatenate([first, second], axis=0)

    active = of(0)
    rank = ranks(active)
    offset = jnp.zeros((2 * Z, T), i32)
    even = jnp.zeros((2 * Z, T), i32)
    counts = [of(1 + l).astype(i32) for l in range(LAYERS)]
    for l, n in enumerate(counts):
        offset += jnp.where(l < rep, n & 7, 0)
        even = jnp.where(l == rep, (n >> 3) << 3, even)
    cls = jnp.where(rank < even, rank, offset + rank - even) & 7
    place_ref[0] = jnp.where(active > 0, cls, -1)
    place_ref[1] = jnp.minimum(rank >> 3, BASE - 1)

    lane = iota((1, T), 1)
    for k in range(2):
        spread = []
        for n in counts:
            at = jnp.zeros((1, T), i32)
            for z in range(Z):
                at = jnp.where((lane >> 4) == z, n[k * Z + z : k * Z + z + 1], at)
            spread.append(at)
        for b in range(2):
            for l, (start, _, _, _) in enumerate(shares(spread, 2 * rep + b)):
                source = SHARE * ((lane >> 4) & 3) + start + (lane & (BASE - 1))
                route_ref[(l * 2 + k) * 2 + b : (l * 2 + k) * 2 + b + 1, :] = source & (T - 1)


def route_kernel(route_ref, sums_ref, out_ref):
    low = iota((64, T), 1) < T // 2
    for k in range(2):
        for b in range(2):
            halves = [sums_ref[k, b, :, h * T : (h + 1) * T] for h in range(2)]
            for l in range(LAYERS):
                row = (l * 2 + k) * 2 + b
                source = jnp.broadcast_to(route_ref[row : row + 1, :], (64, T))
                first, second = (jnp.take_along_axis(x, source, axis=1) for x in halves)
                out_ref[l, k, b] = jnp.where(low, first, second)


def final_kernel(place_ref, sums_ref, residual_ref, out_ref):
    for z in range(Z):
        for k in range(2):
            j = k * Z + z
            own = jnp.broadcast_to(place_ref[0, j : j + 1, :], (64, T))
            lane = BASE * z + jnp.broadcast_to(place_ref[1, j : j + 1, :], (64, T))
            ladder = jnp.zeros((64, T), f32)
            for q in range(CLASSES):
                here = jnp.take_along_axis(sums_ref[q // 2, k, q % 2], lane, axis=1)
                ladder = jnp.where(own == q, here, ladder)
            at = (z * 2 + k) * T
            old = residual_ref[:, at : at + T].astype(f32)
            out_ref[:, at : at + T] = (old + ladder).astype(bf16)


VMEM = pl.BlockSpec(memory_space=pltpu.VMEM)
HBM = pl.BlockSpec(memory_space=pltpu.HBM)
MIB = 2**20


def call(kernel, shape, dtype, *args, far=0, scratch=(), limit=8, flops=0):
    return pl.pallas_call(
        kernel,
        out_shape=[jax.ShapeDtypeStruct(one, dtype) for one in shape]
        if isinstance(shape, list)
        else jax.ShapeDtypeStruct(shape, dtype),
        in_specs=[VMEM] * (len(args) - far) + [HBM] * far,
        out_specs=[VMEM] * len(shape) if isinstance(shape, list) else VMEM,
        scratch_shapes=scratch,
        compiler_params=pltpu.CompilerParams(vmem_limit_bytes=limit and limit * MIB),
        cost_estimate=pl.CostEstimate(flops=flops, bytes_accessed=2**21, transcendentals=0),
    )(*args)


def step(amplitudes, pair_irrep, integrals, residual_in):
    swap = [(0, 1), (1, 0)]

    packed = call(pack_kernel, (LAYERS, SEND, KD), bf16, pair_irrep, amplitudes[0], limit=None, flops=2**26)
    got = lax.all_to_all(packed, "rep", 0, 0, tiled=True)
    shared, info = call(share_kernel, [(2, Z, SHARE, KD), (1, 8, T)], bf16, got, flops=2**26)
    gathered = lax.all_to_all(
        shared.reshape(2 * Z, SHARE, KD), ("b", "z"), 0, 0, tiled=True
    ).reshape(2, Z * SHARE, KD)
    for step in (1, 2, 4):
        info = jnp.concatenate([info, lax.ppermute(info, "z", [(z, z ^ step) for z in range(Z)])])

    other = lax.ppermute(integrals, "b", swap)
    across = lax.ppermute(integrals, "k", swap)
    across_other = lax.ppermute(other, "k", swap)

    partial = call(
        ladder_kernel,
        (2, 512, Z * SHARE),
        f32,
        integrals,
        other,
        gathered,
        across,
        across_other,
        far=2,
        scratch=[
            pltpu.VMEM((512, KD), bf16),
            pltpu.VMEM((512, KD), bf16),
            pltpu.SemaphoreType.DMA((2,)),
        ],
        limit=49,
        flops=2**30,
    )

    sent = partial.astype(jnp.float16).reshape(16, 64, Z * SHARE)
    parts = lax.all_to_all(sent, ("k", "g", "b"), 0, 0, tiled=True)
    sums = jnp.sum(parts.reshape(2, 4, 2, 64, Z * SHARE).astype(f32), axis=1)

    info_across = lax.ppermute(info, "k", swap)
    place, route = call(
        plan_kernel, [(2, 2 * Z, T), (16, T)], i32, jnp.stack([info, info_across]), flops=2**20
    )
    routed = call(route_kernel, (LAYERS, 2, 2, 64, T), f32, route, sums, flops=2**24)
    owned = lax.all_to_all(routed, "rep", 0, 0, tiled=True)
    out = call(final_kernel, (64, 2048), bf16, place, owned, residual_in[0].T, flops=2**26)
    return out.T[None]


def solution(mesh):
    devices = mesh.devices.reshape(8, 2, 4, 2, 4)
    split = Mesh(devices, ("z", "k", "g", "b", "rep"))
    ab, cd = ("z", "k"), ("g", "b")
    return jax.shard_map(
        step,
        mesh=split,
        in_specs=(P("rep", ab, cd), P("rep", ab), P(ab, cd), P("rep", None, ab + cd)),
        out_specs=P("rep", None, ab + cd),
        check_vma=False,
    )
```

```python
import jax
import jax.numpy as jnp
from jax import lax
from jax.experimental import pallas as pl
from jax.experimental.pallas import tpu as pltpu
from jax.sharding import Mesh, PartitionSpec as P


LAYERS = 4
T = 128
KD = 1024
CLASSES = 8
BASE = 16
REST = 2 * BASE
SEND = REST + 8
SHARE = 32
Z = 8
i32, f32, bf16 = jnp.int32, jnp.float32, jnp.bfloat16


def iota(shape, dim):
    return lax.broadcasted_iota(i32, shape, dim)


def ranks(active):
    before = (iota((T, T), 0) < iota((T, T), 1)).astype(bf16)
    return jnp.dot(active.astype(bf16), before, preferred_element_type=f32).astype(i32)


def pack_kernel(labels_ref, rows_far, out_ref, rows_ref, sem):
    rows_in = pltpu.make_async_copy(rows_far, rows_ref, sem)
    rows_in.start()
    active = jnp.broadcast_to(labels_ref[...] == 0, (8, T)).astype(i32).astype(f32)
    rank = jnp.where(active[:1] > 0, ranks(active)[:1], -1)
    count = jnp.sum(active, axis=1, keepdims=True).astype(i32)[:1]
    even = (count >> 3) << 3
    slot = iota((SEND, T), 0)
    lane = iota((SEND, KD), 1)
    srow = iota((SEND, KD), 0)
    flags = jnp.concatenate([active[:1]] * (KD // T), axis=1)
    info = jnp.where(lane < T, flags, count.astype(f32))
    hots = []
    for rep in range(LAYERS):
        shared = 8 * (slot & (BASE - 1)) + 2 * rep + (slot >> 4)
        rest = even + slot - REST
        target = jnp.where(slot < REST, shared, rest)
        bound = jnp.where(slot < REST, even, jnp.where(slot < SEND - 1, count, 0))
        hots.append(((rank == target) & (target < bound)).astype(f32).astype(bf16))
    rows_in.wait()
    for rep, hot in enumerate(hots):
        picked = jnp.dot(hot, rows_ref[...], preferred_element_type=f32)
        out_ref[rep] = jnp.where(srow == SEND - 1, info, picked).astype(bf16)


def shares(counts, q):
    parts, start, offset = [], jnp.zeros_like(counts[0]), jnp.zeros_like(counts[0])
    for n in counts:
        rem = n & 7
        extra = (q - offset) & 7
        length = (n >> 3) + (extra < rem).astype(i32)
        parts.append((start, length, n >> 3, extra))
        start, offset = start + length, offset + rem
    return parts


def share_kernel(got_ref, out_ref, info_ref):
    rep = lax.axis_index("rep")
    counts = [got_ref[l, SEND - 1 : SEND, T : 2 * T].astype(f32).astype(i32) for l in range(LAYERS)]
    row = iota((8, T), 0)
    info = jnp.zeros((8, T), f32)
    for l in range(LAYERS):
        mine = got_ref[l, SEND - 1 : SEND, :T].astype(f32)
        info = jnp.where((row == 0) & (rep == l), mine, info)
        info = jnp.where(row == 1 + l, counts[l].astype(f32), info)
    info_ref[0] = info.astype(bf16)
    s = iota((SHARE, SEND), 0)
    slot = iota((SHARE, SEND), 1)
    for b in range(2):
        total = jnp.zeros((SHARE, KD), f32)
        for l, parts in enumerate(shares(counts, 2 * rep + b)):
            start, length, base, extra = (v[:, :SEND] for v in parts)
            i = s - start
            inside = (i >= 0) & (i < length)
            want = jnp.where(i < base, BASE * b + i, REST + extra)
            hot = (inside & (slot == want)).astype(f32).astype(bf16)
            total += jnp.dot(hot, got_ref[l], preferred_element_type=f32)
        for z in range(Z):
            out_ref[b, z] = total.astype(bf16)


def ladder_kernel(own_ref, pair_ref, got_ref, across_far, across_pair_far, out_ref, *scratch):
    across_ref, across_pair_ref, sems = scratch
    own, pair = lax.axis_index("k"), lax.axis_index("b")
    halves = [pl.ds(at, 256) for at in (0, 256)]
    moves = [
        (source.at[rows], target.at[rows])
        for rows in halves
        for source, target in ((across_far, across_ref), (across_pair_far, across_pair_ref))
    ]
    copies = [pltpu.make_async_copy(*move, sems.at[n]) for n, move in enumerate(moves)]
    for copy in copies:
        copy.start()

    def part(piece, half):
        dims = (((1,), (1,)), ((), ()))
        return lax.dot_general(piece, got_ref[half], dims, preferred_element_type=f32)

    out_ref[own] = part(own_ref[...], pair) + part(pair_ref[...], 1 - pair)
    for n, rows in enumerate(halves):
        copies[2 * n].wait()
        copies[2 * n + 1].wait()
        far = part(across_ref[rows, :], pair) + part(across_pair_ref[rows, :], 1 - pair)
        out_ref[1 - own, rows, :] = far


def plan_kernel(info_ref, place_ref, route_ref):
    rep, own, here = lax.axis_index("rep"), lax.axis_index("k"), lax.axis_index("z")

    def of(r):
        entries = [here ^ z for z in range(Z)]
        at_core = [
            jnp.concatenate([info_ref[s, e, r : r + 1, :].astype(f32) for e in entries], axis=0)
            for s in range(2)
        ]
        first = jnp.where(own == 0, at_core[0], at_core[1])
        second = jnp.where(own == 0, at_core[1], at_core[0])
        return jnp.concatenate([first, second], axis=0)

    active = of(0)
    rank = ranks(active)
    offset = jnp.zeros((2 * Z, T), i32)
    even = jnp.zeros((2 * Z, T), i32)
    counts = [of(1 + l).astype(i32) for l in range(LAYERS)]
    for l, n in enumerate(counts):
        offset += jnp.where(l < rep, n & 7, 0)
        even = jnp.where(l == rep, (n >> 3) << 3, even)
    cls = jnp.where(rank < even, rank, offset + rank - even) & 7
    place_ref[0] = jnp.where(active > 0, cls, -1)
    place_ref[1] = jnp.minimum(rank >> 3, BASE - 1)

    lane = iota((1, T), 1)
    for k in range(2):
        spread = []
        for n in counts:
            at = jnp.zeros((1, T), i32)
            for z in range(Z):
                at = jnp.where((lane >> 4) == z, n[k * Z + z : k * Z + z + 1], at)
            spread.append(at)
        for b in range(2):
            for l, (start, _, _, _) in enumerate(shares(spread, 2 * rep + b)):
                source = SHARE * ((lane >> 4) & 3) + start + (lane & (BASE - 1))
                route_ref[(l * 2 + k) * 2 + b : (l * 2 + k) * 2 + b + 1, :] = source & (T - 1)


def route_kernel(route_ref, sums_ref, out_ref):
    low = iota((64, T), 1) < T // 2
    for k in range(2):
        for b in range(2):
            halves = [sums_ref[k, b, :, h * T : (h + 1) * T] for h in range(2)]
            for l in range(LAYERS):
                row = (l * 2 + k) * 2 + b
                source = jnp.broadcast_to(route_ref[row : row + 1, :], (64, T))
                first, second = (jnp.take_along_axis(x, source, axis=1) for x in halves)
                out_ref[l, k, b] = jnp.where(low, first, second)


def final_kernel(place_ref, sums_ref, residual_ref, out_ref):
    for z in range(Z):
        for k in range(2):
            j = k * Z + z
            own = jnp.broadcast_to(place_ref[0, j : j + 1, :], (64, T))
            lane = BASE * z + jnp.broadcast_to(place_ref[1, j : j + 1, :], (64, T))
            ladder = jnp.zeros((64, T), f32)
            for q in range(CLASSES):
                here = jnp.take_along_axis(sums_ref[q // 2, k, q % 2], lane, axis=1)
                ladder = jnp.where(own == q, here, ladder)
            at = (z * 2 + k) * T
            old = residual_ref[:, at : at + T].astype(f32)
            out_ref[:, at : at + T] = (old + ladder).astype(bf16)


VMEM = pl.BlockSpec(memory_space=pltpu.VMEM)
HBM = pl.BlockSpec(memory_space=pltpu.HBM)
MIB = 2**20


def call(kernel, shape, dtype, *args, far=0, scratch=(), limit=8, flops=0):
    return pl.pallas_call(
        kernel,
        out_shape=[jax.ShapeDtypeStruct(one, dtype) for one in shape]
        if isinstance(shape, list)
        else jax.ShapeDtypeStruct(shape, dtype),
        in_specs=[VMEM] * (len(args) - far) + [HBM] * far,
        out_specs=[VMEM] * len(shape) if isinstance(shape, list) else VMEM,
        scratch_shapes=scratch,
        compiler_params=pltpu.CompilerParams(vmem_limit_bytes=limit and limit * MIB),
        cost_estimate=pl.CostEstimate(flops=flops, bytes_accessed=2**21, transcendentals=0),
    )(*args)


def step(amplitudes, pair_irrep, integrals, residual_in):
    swap = [(0, 1), (1, 0)]

    packed = call(
        pack_kernel,
        (LAYERS, SEND, KD),
        bf16,
        pair_irrep,
        amplitudes[0],
        far=1,
        scratch=[pltpu.VMEM((T, KD), bf16), pltpu.SemaphoreType.DMA],
        limit=None,
        flops=2**26,
    )
    got = lax.all_to_all(packed, "rep", 0, 0, tiled=True)
    shared, info = call(share_kernel, [(2, Z, SHARE, KD), (1, 8, T)], bf16, got, flops=2**26)
    gathered = lax.all_to_all(
        shared.reshape(2 * Z, SHARE, KD), ("b", "z"), 0, 0, tiled=True
    ).reshape(2, Z * SHARE, KD)
    near = [info]
    for step in (1, 2, 3):
        near.append(lax.ppermute(info, "z", [(z, z ^ step) for z in range(Z)]))
    info = jnp.concatenate(near)
    info = jnp.concatenate([info, lax.ppermute(info, "z", [(z, z ^ 4) for z in range(Z)])])

    other = lax.ppermute(integrals, "b", swap)
    across = lax.ppermute(integrals, "k", swap)
    across_other = lax.ppermute(other, "k", swap)

    partial = call(
        ladder_kernel,
        (2, 512, Z * SHARE),
        f32,
        integrals,
        other,
        gathered,
        across,
        across_other,
        far=2,
        scratch=[
            pltpu.VMEM((512, KD), bf16),
            pltpu.VMEM((512, KD), bf16),
            pltpu.SemaphoreType.DMA((4,)),
        ],
        limit=49,
        flops=2**30,
    )

    sent = partial.astype(jnp.float16).reshape(16, 64, Z * SHARE)
    parts = lax.all_to_all(sent, ("k", "g", "b"), 0, 0, tiled=True)
    sums = jnp.sum(parts.reshape(2, 4, 2, 64, Z * SHARE).astype(f32), axis=1)

    info_across = lax.ppermute(info, "k", swap)
    place, route = call(
        plan_kernel, [(2, 2 * Z, T), (16, T)], i32, jnp.stack([info, info_across]), flops=2**20
    )
    routed = call(route_kernel, (LAYERS, 2, 2, 64, T), f32, route, sums, flops=2**24)
    owned = lax.all_to_all(routed, "rep", 0, 0, tiled=True)
    out = call(final_kernel, (64, 2048), bf16, place, owned, residual_in[0].T, flops=2**26)
    return out.T[None]


def solution(mesh):
    devices = mesh.devices.reshape(8, 2, 4, 2, 4)
    split = Mesh(devices, ("z", "k", "g", "b", "rep"))
    ab, cd = ("z", "k"), ("g", "b")
    return jax.shard_map(
        step,
        mesh=split,
        in_specs=(P("rep", ab, cd), P("rep", ab), P(ab, cd), P("rep", None, ab + cd)),
        out_specs=P("rep", None, ab + cd),
        check_vma=False,
    )
```

```python
import jax
import jax.numpy as jnp
from jax import lax
from jax.experimental import pallas as pl
from jax.experimental.pallas import tpu as pltpu
from jax.sharding import Mesh, PartitionSpec as P


LAYERS = 4
T = 128
KD = 1024
CLASSES = 8
BASE = 16
REST = 2 * BASE
SEND = REST + 8
SHARE = 32
Z = 8
i32, f32, bf16 = jnp.int32, jnp.float32, jnp.bfloat16


def iota(shape, dim):
    return lax.broadcasted_iota(i32, shape, dim)


def ranks(active):
    before = (iota((T, T), 0) < iota((T, T), 1)).astype(bf16)
    return jnp.dot(active.astype(bf16), before, preferred_element_type=f32).astype(i32)


def pack_kernel(labels_ref, rows_ref, out_ref):
    active = jnp.broadcast_to(labels_ref[...] == 0, (8, T)).astype(i32).astype(f32)
    rank = jnp.where(active[:1] > 0, ranks(active)[:1], -1)
    count = jnp.sum(active, axis=1, keepdims=True).astype(i32)[:1]
    even = (count >> 3) << 3
    rows = rows_ref[...]
    slot = iota((SEND, T), 0)
    lane = iota((SEND, KD), 1)
    srow = iota((SEND, KD), 0)
    flags = jnp.concatenate([active[:1]] * (KD // T), axis=1)
    info = jnp.where(lane < T, flags, count.astype(f32))
    for rep in range(LAYERS):
        shared = 8 * (slot & (BASE - 1)) + 2 * rep + (slot >> 4)
        rest = even + slot - REST
        target = jnp.where(slot < REST, shared, rest)
        bound = jnp.where(slot < REST, even, jnp.where(slot < SEND - 1, count, 0))
        hot = ((rank == target) & (target < bound)).astype(f32).astype(bf16)
        picked = jnp.dot(hot, rows, preferred_element_type=f32)
        out_ref[rep] = jnp.where(srow == SEND - 1, info, picked).astype(bf16)


def shares(counts, q):
    parts, start, offset = [], jnp.zeros_like(counts[0]), jnp.zeros_like(counts[0])
    for n in counts:
        rem = n & 7
        extra = (q - offset) & 7
        length = (n >> 3) + (extra < rem).astype(i32)
        parts.append((start, length, n >> 3, extra))
        start, offset = start + length, offset + rem
    return parts


def share_kernel(got_ref, out_ref, info_ref):
    rep = lax.axis_index("rep")
    counts = [got_ref[l, SEND - 1 : SEND, T : 2 * T].astype(f32).astype(i32) for l in range(LAYERS)]
    row = iota((8, T), 0)
    info = jnp.zeros((8, T), f32)
    for l in range(LAYERS):
        mine = got_ref[l, SEND - 1 : SEND, :T].astype(f32)
        info = jnp.where((row == 0) & (rep == l), mine, info)
        info = jnp.where(row == 1 + l, counts[l].astype(f32), info)
    info_ref[0] = info.astype(bf16)
    s = iota((SHARE, SEND), 0)
    slot = iota((SHARE, SEND), 1)
    for b in range(2):
        total = jnp.zeros((SHARE, KD), f32)
        for l, parts in enumerate(shares(counts, 2 * rep + b)):
            start, length, base, extra = (v[:, :SEND] for v in parts)
            i = s - start
            inside = (i >= 0) & (i < length)
            want = jnp.where(i < base, BASE * b + i, REST + extra)
            hot = (inside & (slot == want)).astype(f32).astype(bf16)
            total += jnp.dot(hot, got_ref[l], preferred_element_type=f32)
        for z in range(Z):
            out_ref[b, z] = total.astype(bf16)


def ladder_kernel(own_ref, pair_ref, got_ref, across_far, across_pair_far, out_ref, *scratch):
    across_ref, across_pair_ref, sems = scratch
    own, pair = lax.axis_index("k"), lax.axis_index("b")
    moves = ((across_far, across_ref), (across_pair_far, across_pair_ref))
    copies = [pltpu.make_async_copy(*move, sems.at[n]) for n, move in enumerate(moves)]
    for copy in copies:
        copy.start()

    def part(piece, half):
        dims = (((1,), (1,)), ((), ()))
        return lax.dot_general(piece[...], got_ref[half], dims, preferred_element_type=f32)

    out_ref[own] = part(own_ref, pair) + part(pair_ref, 1 - pair)
    copies[0].wait()
    far = part(across_ref, pair)
    copies[1].wait()
    out_ref[1 - own] = far + part(across_pair_ref, 1 - pair)


def plan_kernel(info_ref, place_ref, route_ref):
    rep, own, here = lax.axis_index("rep"), lax.axis_index("k"), lax.axis_index("z")

    def of(r):
        entries = [here ^ z for z in range(Z)]
        at_core = [
            jnp.concatenate([info_ref[s, e, r : r + 1, :].astype(f32) for e in entries], axis=0)
            for s in range(2)
        ]
        first = jnp.where(own == 0, at_core[0], at_core[1])
        second = jnp.where(own == 0, at_core[1], at_core[0])
        return jnp.concatenate([first, second], axis=0)

    active = of(0)
    rank = ranks(active)
    offset = jnp.zeros((2 * Z, T), i32)
    even = jnp.zeros((2 * Z, T), i32)
    counts = [of(1 + l).astype(i32) for l in range(LAYERS)]
    for l, n in enumerate(counts):
        offset += jnp.where(l < rep, n & 7, 0)
        even = jnp.where(l == rep, (n >> 3) << 3, even)
    cls = jnp.where(rank < even, rank, offset + rank - even) & 7
    place_ref[0] = jnp.where(active > 0, cls, -1)
    place_ref[1] = jnp.minimum(rank >> 3, BASE - 1)

    lane = iota((1, T), 1)
    for k in range(2):
        spread = []
        for n in counts:
            at = jnp.zeros((1, T), i32)
            for z in range(Z):
                at = jnp.where((lane >> 4) == z, n[k * Z + z : k * Z + z + 1], at)
            spread.append(at)
        for b in range(2):
            for l, (start, _, _, _) in enumerate(shares(spread, 2 * rep + b)):
                source = SHARE * ((lane >> 4) & 3) + start + (lane & (BASE - 1))
                route_ref[(l * 2 + k) * 2 + b : (l * 2 + k) * 2 + b + 1, :] = source & (T - 1)


def route_kernel(route_ref, sums_ref, out_ref):
    low = iota((64, T), 1) < T // 2
    for k in range(2):
        for b in range(2):
            halves = [sums_ref[k, b, :, h * T : (h + 1) * T] for h in range(2)]
            for l in range(LAYERS):
                row = (l * 2 + k) * 2 + b
                source = jnp.broadcast_to(route_ref[row : row + 1, :], (64, T))
                first, second = (jnp.take_along_axis(x, source, axis=1) for x in halves)
                out_ref[l, k, b] = jnp.where(low, first, second)


def final_kernel(place_ref, sums_ref, residual_ref, out_ref):
    for z in range(Z):
        for k in range(2):
            j = k * Z + z
            own = jnp.broadcast_to(place_ref[0, j : j + 1, :], (64, T))
            lane = BASE * z + jnp.broadcast_to(place_ref[1, j : j + 1, :], (64, T))
            ladder = jnp.zeros((64, T), f32)
            for q in range(CLASSES):
                here = jnp.take_along_axis(sums_ref[q // 2, k, q % 2], lane, axis=1)
                ladder = jnp.where(own == q, here, ladder)
            at = (z * 2 + k) * T
            old = residual_ref[:, at : at + T].astype(f32)
            out_ref[:, at : at + T] = (old + ladder).astype(bf16)


VMEM = pl.BlockSpec(memory_space=pltpu.VMEM)
HBM = pl.BlockSpec(memory_space=pltpu.HBM)
MIB = 2**20


def call(kernel, shape, dtype, *args, far=0, scratch=(), limit=8, flops=0):
    return pl.pallas_call(
        kernel,
        out_shape=[jax.ShapeDtypeStruct(one, dtype) for one in shape]
        if isinstance(shape, list)
        else jax.ShapeDtypeStruct(shape, dtype),
        in_specs=[VMEM] * (len(args) - far) + [HBM] * far,
        out_specs=[VMEM] * len(shape) if isinstance(shape, list) else VMEM,
        scratch_shapes=scratch,
        compiler_params=pltpu.CompilerParams(vmem_limit_bytes=limit and limit * MIB),
        cost_estimate=pl.CostEstimate(flops=flops, bytes_accessed=2**21, transcendentals=0),
    )(*args)


def step(amplitudes, pair_irrep, integrals, residual_in):
    swap = [(0, 1), (1, 0)]

    packed = call(pack_kernel, (LAYERS, SEND, KD), bf16, pair_irrep, amplitudes[0], limit=None, flops=2**26)
    got = lax.all_to_all(packed, "rep", 0, 0, tiled=True)
    shared, info = call(share_kernel, [(2, Z, SHARE, KD), (1, 8, T)], bf16, got, flops=2**26)
    gathered = lax.all_to_all(
        shared.reshape(2 * Z, SHARE, KD), ("b", "z"), 0, 0, tiled=True
    ).reshape(2, Z * SHARE, KD)
    near = [info]
    for step in (1, 2, 3):
        near.append(lax.ppermute(info, "z", [(z, z ^ step) for z in range(Z)]))
    info = jnp.concatenate(near)
    info = jnp.concatenate([info, lax.ppermute(info, "z", [(z, z ^ 4) for z in range(Z)])])

    other = lax.ppermute(integrals, "b", swap)
    across = lax.ppermute(integrals, "k", swap)
    across_other = lax.ppermute(other, "k", swap)

    partial = call(
        ladder_kernel,
        (2, 512, Z * SHARE),
        f32,
        integrals,
        other,
        gathered,
        across,
        across_other,
        far=2,
        scratch=[
            pltpu.VMEM((512, KD), bf16),
            pltpu.VMEM((512, KD), bf16),
            pltpu.SemaphoreType.DMA((2,)),
        ],
        limit=48,
        flops=2**30,
    )

    sent = partial.astype(jnp.float16).reshape(16, 64, Z * SHARE)
    parts = lax.all_to_all(sent, ("k", "g", "b"), 0, 0, tiled=True)
    sums = jnp.sum(parts.reshape(2, 4, 2, 64, Z * SHARE).astype(f32), axis=1)

    info_across = lax.ppermute(info, "k", swap)
    place, route = call(
        plan_kernel, [(2, 2 * Z, T), (16, T)], i32, jnp.stack([info, info_across]), flops=2**20
    )
    routed = call(route_kernel, (LAYERS, 2, 2, 64, T), f32, route, sums, flops=2**24)
    owned = lax.all_to_all(routed, "rep", 0, 0, tiled=True)
    out = call(final_kernel, (64, 2048), bf16, place, owned, residual_in[0].T, flops=2**26)
    return out.T[None]


def solution(mesh):
    devices = mesh.devices.reshape(8, 2, 4, 2, 4)
    split = Mesh(devices, ("z", "k", "g", "b", "rep"))
    ab, cd = ("z", "k"), ("g", "b")
    return jax.shard_map(
        step,
        mesh=split,
        in_specs=(P("rep", ab, cd), P("rep", ab), P(ab, cd), P("rep", None, ab + cd)),
        out_specs=P("rep", None, ab + cd),
        check_vma=False,
    )
```

```python
import jax
import jax.numpy as jnp
from jax import lax
from jax.experimental import pallas as pl
from jax.experimental.pallas import tpu as pltpu
from jax.sharding import Mesh, PartitionSpec as P


LAYERS = 4
T = 128
KD = 1024
CLASSES = 8
BASE = 16
REST = 2 * BASE
SEND = REST + 8
SHARE = 32
Z = 8
i32, f32, bf16 = jnp.int32, jnp.float32, jnp.bfloat16


def iota(shape, dim):
    return lax.broadcasted_iota(i32, shape, dim)


def ranks(active):
    before = (iota((T, T), 0) < iota((T, T), 1)).astype(bf16)
    return jnp.dot(active.astype(bf16), before, preferred_element_type=f32).astype(i32)


def pack_kernel(labels_ref, rows_ref, out_ref):
    active = jnp.broadcast_to(labels_ref[...] == 0, (8, T)).astype(i32).astype(f32)
    rank = jnp.where(active[:1] > 0, ranks(active)[:1], -1)
    count = jnp.sum(active, axis=1, keepdims=True).astype(i32)[:1]
    even = (count >> 3) << 3
    rows = rows_ref[...]
    slot = iota((SEND, T), 0)
    lane = iota((SEND, KD), 1)
    srow = iota((SEND, KD), 0)
    flags = jnp.concatenate([active[:1]] * (KD // T), axis=1)
    info = jnp.where(lane < T, flags, count.astype(f32))
    for rep in range(LAYERS):
        shared = 8 * (slot & (BASE - 1)) + 2 * rep + (slot >> 4)
        rest = even + slot - REST
        target = jnp.where(slot < REST, shared, rest)
        bound = jnp.where(slot < REST, even, jnp.where(slot < SEND - 1, count, 0))
        hot = ((rank == target) & (target < bound)).astype(f32).astype(bf16)
        picked = jnp.dot(hot, rows, preferred_element_type=f32)
        out_ref[rep] = jnp.where(srow == SEND - 1, info, picked).astype(bf16)


def shares(counts, q):
    parts, start, offset = [], jnp.zeros_like(counts[0]), jnp.zeros_like(counts[0])
    for n in counts:
        rem = n & 7
        extra = (q - offset) & 7
        length = (n >> 3) + (extra < rem).astype(i32)
        parts.append((start, length, n >> 3, extra))
        start, offset = start + length, offset + rem
    return parts


def share_kernel(got_ref, out_ref, info_ref):
    rep = lax.axis_index("rep")
    counts = [got_ref[l, SEND - 1 : SEND, T : 2 * T].astype(f32).astype(i32) for l in range(LAYERS)]
    row = iota((8, T), 0)
    info = jnp.zeros((8, T), f32)
    for l in range(LAYERS):
        mine = got_ref[l, SEND - 1 : SEND, :T].astype(f32)
        info = jnp.where((row == 0) & (rep == l), mine, info)
        info = jnp.where(row == 1 + l, counts[l].astype(f32), info)
    info_ref[0] = info.astype(bf16)
    s = iota((SHARE, SEND), 0)
    slot = iota((SHARE, SEND), 1)
    for b in range(2):
        total = jnp.zeros((SHARE, KD), f32)
        for l, parts in enumerate(shares(counts, 2 * rep + b)):
            start, length, base, extra = (v[:, :SEND] for v in parts)
            i = s - start
            inside = (i >= 0) & (i < length)
            want = jnp.where(i < base, BASE * b + i, REST + extra)
            hot = (inside & (slot == want)).astype(f32).astype(bf16)
            total += jnp.dot(hot, got_ref[l], preferred_element_type=f32)
        for z in range(Z):
            out_ref[b, z] = total.astype(bf16)


def ladder_kernel(own_ref, pair_ref, got_ref, across_far, across_pair_far, out_ref, *scratch):
    across_ref, across_pair_ref, sems = scratch
    own, pair = lax.axis_index("k"), lax.axis_index("b")
    moves = ((across_far, across_ref), (across_pair_far, across_pair_ref))
    copies = [pltpu.make_async_copy(*move, sems.at[n]) for n, move in enumerate(moves)]
    for copy in copies:
        copy.start()

    def part(piece, half):
        dims = (((1,), (1,)), ((), ()))
        return lax.dot_general(piece[...], got_ref[half], dims, preferred_element_type=f32)

    out_ref[own] = part(own_ref, pair) + part(pair_ref, 1 - pair)
    copies[0].wait()
    far = part(across_ref, pair)
    copies[1].wait()
    out_ref[1 - own] = far + part(across_pair_ref, 1 - pair)


def by_index(info_ref, r):
    own, here = lax.axis_index("k"), lax.axis_index("z")
    entries = [here ^ z for z in range(Z)]
    at_core = [
        jnp.concatenate([info_ref[s, e, r : r + 1, :].astype(f32) for e in entries], axis=0)
        for s in range(2)
    ]
    first = jnp.where(own == 0, at_core[0], at_core[1])
    second = jnp.where(own == 0, at_core[1], at_core[0])
    return jnp.concatenate([first, second], axis=0)


def place_kernel(info_ref, place_ref):
    rep = lax.axis_index("rep")
    active = by_index(info_ref, 0)
    rank = ranks(active)
    offset = jnp.zeros((2 * Z, T), i32)
    even = jnp.zeros((2 * Z, T), i32)
    for l in range(LAYERS):
        n = by_index(info_ref, 1 + l).astype(i32)
        offset += jnp.where(l < rep, n & 7, 0)
        even = jnp.where(l == rep, (n >> 3) << 3, even)
    cls = jnp.where(rank < even, rank, offset + rank - even) & 7
    place_ref[0] = jnp.where(active > 0, cls, -1)
    place_ref[1] = jnp.minimum(rank >> 3, BASE - 1)


def plan_kernel(info_ref, route_ref):
    rep = lax.axis_index("rep")
    counts = [by_index(info_ref, 1 + l).astype(i32) for l in range(LAYERS)]
    lane = iota((1, T), 1)
    for k in range(2):
        spread = []
        for n in counts:
            at = jnp.zeros((1, T), i32)
            for z in range(Z):
                at = jnp.where((lane >> 4) == z, n[k * Z + z : k * Z + z + 1], at)
            spread.append(at)
        for b in range(2):
            for l, (start, _, _, _) in enumerate(shares(spread, 2 * rep + b)):
                source = SHARE * ((lane >> 4) & 3) + start + (lane & (BASE - 1))
                route_ref[(l * 2 + k) * 2 + b : (l * 2 + k) * 2 + b + 1, :] = source & (T - 1)


def route_kernel(route_ref, sums_ref, out_ref):
    low = iota((64, T), 1) < T // 2
    for k in range(2):
        for b in range(2):
            halves = [sums_ref[k, b, :, h * T : (h + 1) * T] for h in range(2)]
            for l in range(LAYERS):
                row = (l * 2 + k) * 2 + b
                source = jnp.broadcast_to(route_ref[row : row + 1, :], (64, T))
                first, second = (jnp.take_along_axis(x, source, axis=1) for x in halves)
                out_ref[l, k, b] = jnp.where(low, first, second)


def final_kernel(place_ref, sums_ref, residual_ref, out_ref):
    for z in range(Z):
        for k in range(2):
            j = k * Z + z
            own = jnp.broadcast_to(place_ref[0, j : j + 1, :], (64, T))
            lane = BASE * z + jnp.broadcast_to(place_ref[1, j : j + 1, :], (64, T))
            ladder = jnp.zeros((64, T), f32)
            for q in range(CLASSES):
                here = jnp.take_along_axis(sums_ref[q // 2, k, q % 2], lane, axis=1)
                ladder = jnp.where(own == q, here, ladder)
            at = (z * 2 + k) * T
            old = residual_ref[:, at : at + T].astype(f32)
            out_ref[:, at : at + T] = (old + ladder).astype(bf16)


VMEM = pl.BlockSpec(memory_space=pltpu.VMEM)
HBM = pl.BlockSpec(memory_space=pltpu.HBM)
MIB = 2**20


def call(kernel, shape, dtype, *args, far=0, scratch=(), limit=8, flops=0):
    return pl.pallas_call(
        kernel,
        out_shape=[jax.ShapeDtypeStruct(one, dtype) for one in shape]
        if isinstance(shape, list)
        else jax.ShapeDtypeStruct(shape, dtype),
        in_specs=[VMEM] * (len(args) - far) + [HBM] * far,
        out_specs=[VMEM] * len(shape) if isinstance(shape, list) else VMEM,
        scratch_shapes=scratch,
        compiler_params=pltpu.CompilerParams(vmem_limit_bytes=limit and limit * MIB),
        cost_estimate=pl.CostEstimate(flops=flops, bytes_accessed=2**21, transcendentals=0),
    )(*args)


def step(amplitudes, pair_irrep, integrals, residual_in):
    swap = [(0, 1), (1, 0)]

    packed = call(pack_kernel, (LAYERS, SEND, KD), bf16, pair_irrep, amplitudes[0], limit=None, flops=2**26)
    got = lax.all_to_all(packed, "rep", 0, 0, tiled=True)
    shared, info = call(share_kernel, [(2, Z, SHARE, KD), (1, 8, T)], bf16, got, flops=2**26)
    gathered = lax.all_to_all(
        shared.reshape(2 * Z, SHARE, KD), ("b", "z"), 0, 0, tiled=True
    ).reshape(2, Z * SHARE, KD)
    near = [info]
    for step in (1, 2, 3):
        near.append(lax.ppermute(info, "z", [(z, z ^ step) for z in range(Z)]))
    info = jnp.concatenate(near)
    info = jnp.concatenate([info, lax.ppermute(info, "z", [(z, z ^ 4) for z in range(Z)])])

    other = lax.ppermute(integrals, "b", swap)
    across = lax.ppermute(integrals, "k", swap)
    across_other = lax.ppermute(other, "k", swap)

    partial = call(
        ladder_kernel,
        (2, 512, Z * SHARE),
        f32,
        integrals,
        other,
        gathered,
        across,
        across_other,
        far=2,
        scratch=[
            pltpu.VMEM((512, KD), bf16),
            pltpu.VMEM((512, KD), bf16),
            pltpu.SemaphoreType.DMA((2,)),
        ],
        limit=49,
        flops=2**30,
    )

    sent = partial.astype(jnp.float16).reshape(16, 64, Z * SHARE)
    parts = lax.all_to_all(sent, ("k", "g", "b"), 0, 0, tiled=True)
    sums = jnp.sum(parts.reshape(2, 4, 2, 64, Z * SHARE).astype(f32), axis=1)

    info_across = lax.ppermute(info, "k", swap)
    infos = jnp.stack([info, info_across])
    route = call(plan_kernel, (16, T), i32, infos, flops=2**20)
    place = call(place_kernel, (2, 2 * Z, T), i32, infos, flops=2**20)
    routed = call(route_kernel, (LAYERS, 2, 2, 64, T), f32, route, sums, flops=2**24)
    owned = lax.all_to_all(routed, "rep", 0, 0, tiled=True)
    out = call(final_kernel, (64, 2048), bf16, place, owned, residual_in[0].T, flops=2**26)
    return out.T[None]


def solution(mesh):
    devices = mesh.devices.reshape(8, 2, 4, 2, 4)
    split = Mesh(devices, ("z", "k", "g", "b", "rep"))
    ab, cd = ("z", "k"), ("g", "b")
    return jax.shard_map(
        step,
        mesh=split,
        in_specs=(P("rep", ab, cd), P("rep", ab), P(ab, cd), P("rep", None, ab + cd)),
        out_specs=P("rep", None, ab + cd),
        check_vma=False,
    )
```
